512 devices in a mesh: dom: 64 (over z, x, core), col: 8 (over y).
Axes of the slice: x: 4, y: 8, z: 8, core: 2. Of those that a mesh axis runs over, the one named last changes fastest.
Arguments:
- feature: bfloat16 [32768, 1024], P('dom', 'col'), may hold values from -6 to 6
- cotangent: bfloat16 [32768, 1024], P('dom', 'col'), may hold values from -6 to 6
- node_type: int32 [32768], P('dom'), may hold values from 0 to 2
- self_gain: float32 [3, 1024], P(None, 'col'), may hold values from 0.1 to 1.9
- weights: bfloat16 [8, 1024, 1024], P(None, 'dom', 'col'), may hold values from -0.1875 to 0.1875
- tile_values: bfloat16 [2048, 128, 128], P('dom'), may hold values from -0.5 to 0.5
- tile_rel: int32 [2048], P('dom'), may hold values from 0 to 7
- tile_src: int32 [2048], P('dom'), may hold values from 0 to 3
- tile_peer: int32 [2048], P('dom'), may hold values from 0 to 63, as said below
- tile_count: int32 [64], P('dom'), may hold values from 24 to 32, as said below
- send_block: int32 [64, 64], P('dom'), may hold values from -1 to 3, as said below
Outputs:
- feature_grad: bfloat16 [32768, 1024], P('dom', 'col')
- weight_grad: bfloat16 [8, 1024, 1024], P(None, None, 'col')
The draws below stay inside these ranges and needn't reach their ends.
Inputs may be any that keep to these rules, and one draw needn't show every extreme that they name: Slots 0 to tile_count - 1 of each partition hold its tiles, the others hold none; some partition uses all 32 slots in every draw. `tile_peer`: the used slots of one partition name distinct owner partitions. send_block[o, p] is at least 0 exactly when some used slot of partition p names o, and then it is that slot's destination block within o.
All inputs are finite; a program needn't handle non-finite values.
Results may differ from the reference program's by a relative error of at most 0.0052.
Values may be sent and summed in bfloat16 or wider, within the bound.
No kernel may reach another device: no remote copies, remote signals or barrier semaphores. Data moves between devices by JAX's collectives and lax.ppermute only.
A program may use at most 64 MiB of HBM per device.

```python
import math
import jax
import jax.numpy as jnp
from jax import lax

D = 1024
RELS = 8
NTYPES = 3
TILE = 128
BLK_DEV = 4
TILES_DEV = 32
NODES = 32768
TILES = 2048
N_DOM = 64


def layout_tables(key):
    base_key = jax.random.fold_in(key, 7)
    key_list = jax.random.split(base_key, N_DOM + 3)
    orders = jax.vmap(lambda single: jax.random.permutation(single, N_DOM))(key_list[:N_DOM]).astype(jnp.int32)
    peer_ids = orders[:, :TILES_DEV]
    lowest = (3 * TILES_DEV + 3) // 4
    used_count = jax.random.randint(key_list[N_DOM], (N_DOM,), lowest, TILES_DEV + 1)
    fullest = jax.random.randint(key_list[N_DOM + 1], (), 0, N_DOM)
    used_count = jnp.where(jnp.arange(N_DOM) == fullest, TILES_DEV, used_count).astype(jnp.int32)
    chosen = jax.random.randint(key_list[N_DOM + 2], (N_DOM, TILES_DEV), 0, BLK_DEV).astype(jnp.int32)
    return (peer_ids, used_count, chosen)


def draw_tile_peer(key, part):
    peer_ids, used_count, chosen = layout_tables(key)
    return peer_ids.reshape(N_DOM * TILES_DEV).astype(jnp.int32)


def draw_tile_count(key, part):
    peer_ids, used_count, chosen = layout_tables(key)
    return used_count


def draw_send_block(key, part):
    peer_ids, used_count, chosen = layout_tables(key)
    is_used = jnp.arange(TILES_DEV)[None, :] < used_count[:, None]
    entries = jnp.where(is_used, chosen, -1).astype(jnp.int32)
    receivers = jnp.broadcast_to(jnp.arange(N_DOM, dtype=jnp.int32)[:, None], (N_DOM, TILES_DEV))
    blank = jnp.full((N_DOM, N_DOM), -1, jnp.int32)
    return blank.at[peer_ids.reshape(-1), receivers.reshape(-1)].max(entries.reshape(-1))


def with_ends(array, stream_key, least, top_value):
    longest = array.shape.index(max(array.shape))
    spots = []
    for shift in (0, 1):
        where = [jax.random.randint(jax.random.fold_in(stream_key, axis), (), 0, length) for axis, length in enumerate(array.shape)]
        where[longest] = (where[longest] + shift) % array.shape[longest]
        spots.append(tuple(where))
    return array.at[spots[0]].set(least).at[spots[1]].set(top_value)


def block_levels(own_key, shape, pieces, low, high):
    loudness = 1.0
    for axis_at, parts in pieces:
        heights = jax.random.uniform(jax.random.fold_in(jax.random.fold_in(own_key, 6), axis_at), (parts,), jnp.float32, low / len(pieces), high / len(pieces))
        loudness = loudness * jnp.repeat(jnp.exp(heights), shape[axis_at] // parts).reshape((-1,) + (1,) * (len(shape) - 1 - axis_at))
    return loudness


def centred(stream_key, extent, deviation, most, cuts=(), kind=jnp.bfloat16):
    loudness = block_levels(stream_key, extent, cuts, -0.22, 0.18) if cuts else 1.0
    drawn = jax.random.normal(stream_key, extent, jnp.float32) * deviation * loudness
    return jnp.minimum(jnp.maximum(drawn, -most), most).astype(kind)


def setup_inputs(seed: int = 0) -> dict:
    keys = jax.random.split(jax.random.key(seed), 12)
    return {
        "feature": centred(keys[0], (NODES, D), 1.0, 6.0, ((0, 64), (1, 8))),
        "cotangent": centred(keys[1], (NODES, D), 1.0, 6.0, ((0, 64), (1, 8))),
        "node_type": with_ends(jax.random.randint(keys[2], (NODES,), 0, NTYPES), jax.random.fold_in(keys[2], 1), 0, NTYPES - 1).astype(jnp.int32),
        "self_gain": jnp.clip(1.0 + 0.18 * jax.random.normal(keys[3], (NTYPES, D), jnp.float32), 0.1, 1.9),
        "weights": centred(keys[4], (RELS, D, D), D ** -0.5, 0.1875, ((1, 64), (2, 8))),
        "tile_values": centred(keys[5], (TILES, TILE, TILE), TILE ** -0.5, 0.5, ((0, 64),)),
        "tile_rel": with_ends(jax.random.randint(keys[6], (TILES,), 0, RELS), jax.random.fold_in(keys[6], 1), 0, RELS - 1).astype(jnp.int32),
        "tile_src": with_ends(jax.random.randint(keys[7], (TILES,), 0, BLK_DEV), jax.random.fold_in(keys[7], 1), 0, BLK_DEV - 1).astype(jnp.int32),
        "tile_peer": draw_tile_peer(jax.random.fold_in(keys[11], 71), 0),
        "tile_count": draw_tile_count(jax.random.fold_in(keys[11], 71), 0),
        "send_block": draw_send_block(jax.random.fold_in(keys[11], 71), 0),
    }


def reference(feature, cotangent, node_type, self_gain, weights, tile_values, tile_rel, tile_src, tile_peer, tile_count, send_block):
    row_count = BLK_DEV * TILE
    grad_blocks = cotangent.reshape(N_DOM * BLK_DEV, TILE, D)
    weight_full = weights.astype(jnp.float32)
    norm_scale = 1.0 / math.sqrt(NODES)

    def per_partition(running, partition):
        first_slot = partition * TILES_DEV
        peer_ids = lax.dynamic_slice_in_dim(tile_peer, first_slot, TILES_DEV)
        rel_ids = lax.dynamic_slice_in_dim(tile_rel, first_slot, TILES_DEV)
        sources = lax.dynamic_slice_in_dim(tile_src, first_slot, TILES_DEV)
        tile_block = lax.dynamic_slice_in_dim(tile_values, first_slot, TILES_DEV, 0)
        used_count = lax.dynamic_index_in_dim(tile_count, partition, 0, keepdims=False)
        send_column = lax.dynamic_index_in_dim(send_block, partition, 1, keepdims=False)
        local_block = jnp.maximum(send_column[peer_ids], 0).astype(jnp.int32)
        target_block = (peer_ids * BLK_DEV + local_block).astype(jnp.int32)
        picked = grad_blocks[target_block]
        contribs = jnp.einsum('tds,tdk->tsk', tile_block.astype(jnp.float32), picked.astype(jnp.float32))
        is_used = jnp.arange(TILES_DEV, dtype=jnp.int32) < used_count
        slot_of = rel_ids * BLK_DEV + sources
        slot_table = ((slot_of[None, :] == jnp.arange(RELS * BLK_DEV, dtype=jnp.int32)[:, None]) & is_used[None, :]).astype(jnp.float32)
        merged = jnp.einsum('mt,tsk->msk', slot_table, contribs, precision=lax.Precision.HIGHEST)
        block_grad = merged.astype(jnp.bfloat16).reshape(RELS, row_count, D).astype(jnp.float32)
        part_feature = lax.dynamic_slice_in_dim(feature, partition * row_count, row_count, 0)
        part_grad = lax.dynamic_slice_in_dim(cotangent, partition * row_count, row_count, 0)
        node_kinds = lax.dynamic_slice_in_dim(node_type, partition * row_count, row_count, 0)
        kind_table = (node_kinds[:, None] == jnp.arange(NTYPES, dtype=jnp.int32)[None, :]).astype(jnp.float32)
        self_gains = jnp.dot(kind_table, self_gain, precision=lax.Precision.HIGHEST)
        combined = jnp.einsum('rnk,rjk->nj', block_grad, weight_full) + part_grad.astype(jnp.float32) * self_gains
        running = running + jnp.einsum('nj,rnk->rjk', part_feature.astype(jnp.float32), block_grad)
        return (running, combined.astype(jnp.bfloat16))
    running, out_rows = lax.scan(per_partition, jnp.zeros((RELS, D, D), jnp.float32), jnp.arange(N_DOM, dtype=jnp.int32))
    feature_grad = out_rows.reshape(NODES, D)
    weight_grad = (running * norm_scale).astype(jnp.bfloat16)
    return (feature_grad, weight_grad)
```

```python
import math

import jax
import jax.numpy as jnp
from jax import lax
from jax.experimental import pallas as pl
from jax.experimental.pallas import tpu as pltpu
from jax.sharding import Mesh, PartitionSpec as P

BF = jnp.bfloat16
F32 = jnp.float32
DOM = ("z", "x", "core")


def cost(flops, nbytes):
    return pl.CostEstimate(flops=flops, bytes_accessed=nbytes, transcendentals=0)


def whole():
    return pl.BlockSpec(memory_space=pltpu.VMEM)


def pick_blocks(wanted, blocks):
    count = wanted.shape[0]
    _, rows, cols = blocks.shape
    group = 16

    def kernel(want_ref, blk_ref, out_ref):
        base = pl.program_id(0) * group
        for i in range(group):
            out_ref[i] = blk_ref[jnp.maximum(want_ref[base + i], 0)]

    return pl.pallas_call(
        kernel,
        out_shape=jax.ShapeDtypeStruct((count, rows, cols), blocks.dtype),
        grid_spec=pltpu.PrefetchScalarGridSpec(
            num_scalar_prefetch=1,
            grid=(count // group,),
            in_specs=[pl.BlockSpec(blocks.shape, lambda i, w: (0, 0, 0))],
            out_specs=pl.BlockSpec((group, rows, cols), lambda i, w: (i, 0, 0)),
        ),
        cost_estimate=cost(0, count * rows * cols * 2),
        name="pick_blocks",
    )(wanted, blocks)


def merge_tiles(peer, slot, count, tiles, incoming, relations, block_count):
    slots, size, _ = tiles.shape
    cols = incoming.shape[2]
    half = relations // 2
    buckets = relations * block_count

    def kernel(peer_ref, slot_ref, count_ref, tile_ref, inc_ref, out_ref, con, acc):
        acc[...] = jnp.zeros_like(acc)
        for t in range(slots):
            con[t] = lax.dot_general(
                tile_ref[t],
                inc_ref[peer_ref[t]],
                (((0,), (0,)), ((), ())),
                preferred_element_type=F32,
            )
        for t in range(slots):
            where = jnp.where(t < count_ref[0], slot_ref[t], buckets)
            acc[where] += con[t]
        for r in range(relations):
            for b in range(block_count):
                out_ref[r // half, b * size : (b + 1) * size, (r % half) * cols : (r % half + 1) * cols] = acc[
                    r * block_count + b
                ].astype(BF)

    smem = pl.BlockSpec(memory_space=pltpu.SMEM)
    return pl.pallas_call(
        kernel,
        out_shape=jax.ShapeDtypeStruct((2, block_count * size, half * cols), BF),
        in_specs=[smem, smem, smem, whole(), whole()],
        out_specs=whole(),
        scratch_shapes=[
            pltpu.VMEM((slots, size, cols), F32),
            pltpu.VMEM((buckets + 1, size, cols), F32),
        ],
        compiler_params=pltpu.CompilerParams(vmem_limit_bytes=24 << 20),
        cost_estimate=cost(2 * slots * size * size * cols, 4 << 20),
        name="merge_tiles",
    )(peer, slot, count, tiles, incoming)


def flip(pieces):
    n = len(pieces)
    rows, cols = pieces[0].shape

    def kernel(*refs):
        out_ref = refs[n]
        for i in range(n):
            out_ref[i] = refs[i][...].T

    return pl.pallas_call(
        kernel,
        out_shape=jax.ShapeDtypeStruct((n, cols, rows), pieces[0].dtype),
        in_specs=[whole()] * n,
        out_specs=whole(),
        cost_estimate=cost(0, 2 * n * rows * cols * 2),
        name="flip",
    )(*pieces)


def fold(parts, scale, copies):
    n, rows, cols = parts.shape
    steps = 4 if rows > 512 else 1
    block = rows // steps

    def kernel(in_ref, out_ref):
        total = in_ref[0].astype(F32)
        for i in range(1, n):
            total = total + in_ref[i].astype(F32)
        if scale is not None:
            total = total * scale
        total = total.astype(BF)
        for i in range(copies):
            out_ref[i] = total

    return pl.pallas_call(
        kernel,
        out_shape=jax.ShapeDtypeStruct((copies, rows, cols), BF),
        grid=(steps,),
        in_specs=[pl.BlockSpec((n, block, cols), lambda i: (0, i, 0))],
        out_specs=pl.BlockSpec((copies, block, cols), lambda i: (0, i, 0)),
        cost_estimate=cost(n * rows * cols, (n + copies) * rows * cols * 2),
        name="fold",
    )(parts)


def weight_terms(which, feature_t, block_grad, relations):
    n, jw, rows = feature_t.shape
    wide = block_grad.shape[2]
    half = relations // 2
    cols = wide // half

    def kernel(which_ref, f_ref, g_ref, out_ref):
        d = jnp.dot(f_ref[0], g_ref[0], preferred_element_type=F32)
        for r in range(half):
            out_ref[r] = d[:, r * cols : (r + 1) * cols]

    return pl.pallas_call(
        kernel,
        out_shape=jax.ShapeDtypeStruct((half, n * jw, cols), F32),
        grid_spec=pltpu.PrefetchScalarGridSpec(
            num_scalar_prefetch=1,
            grid=(n,),
            in_specs=[
                pl.BlockSpec((1, jw, rows), lambda c, w: (c, 0, 0)),
                pl.BlockSpec((1, rows, wide), lambda c, w: (w[0], 0, 0)),
            ],
            out_specs=pl.BlockSpec((half, jw, cols), lambda c, w: (0, lax.rem(w[1] - c + n, n), 0)),
        ),
        cost_estimate=cost(2 * n * jw * rows * wide, 4 << 20),
        name="weight_terms",
    )(which, feature_t, block_grad)


def feature_terms(block_grad, weight_rows, n):
    _, rows, wide = block_grad.shape
    jw = weight_rows.shape[0] // n

    def kernel(g_ref, w_ref, out_ref):
        total = None
        for h in range(2):
            part = lax.dot_general(
                g_ref[h],
                w_ref[:, h * wide : (h + 1) * wide],
                (((1,), (1,)), ((), ())),
                preferred_element_type=F32,
            )
            total = part if total is None else total + part
        out_ref[0] = total

    return pl.pallas_call(
        kernel,
        out_shape=jax.ShapeDtypeStruct((n, rows, jw), F32),
        grid=(n,),
        in_specs=[
            pl.BlockSpec(block_grad.shape, lambda c: (0, 0, 0)),
            pl.BlockSpec((jw, 2 * wide), lambda c: (c, 0)),
        ],
        out_specs=pl.BlockSpec((1, rows, jw), lambda c: (c, 0, 0)),
        cost_estimate=cost(4 * n * jw * rows * wide, 4 << 20),
        name="feature_terms",
    )(block_grad, weight_rows)


def exchange(parts, axis):
    return lax.all_to_all(parts, axis, split_axis=0, concat_axis=0, tiled=True)


def repeat(part, n):
    return jnp.broadcast_to(part[None], (n,) + part.shape)


def body(
    feature,
    cotangent,
    node_type,
    self_gain,
    weights,
    tile_values,
    tile_rel,
    tile_src,
    tile_peer,
    tile_count,
    send_block,
):
    partitions = lax.axis_size(DOM)
    row_count, col_width = cotangent.shape
    tile_size = tile_values.shape[1]
    block_count = row_count // tile_size
    relations, w_rows, _ = weights.shape
    half = relations // 2
    columns = lax.axis_size("y")
    nx = lax.axis_size("x")
    nz = lax.axis_size("z")
    core = lax.axis_index("core").astype(jnp.int32)

    outgoing = pick_blocks(send_block[0], cotangent.reshape(block_count, tile_size, col_width))
    incoming = exchange(outgoing, DOM)
    column = lax.axis_index("y").astype(jnp.int32)
    weight_rows = lax.all_gather(
        weights.transpose(1, 0, 2).reshape(w_rows, relations * col_width), DOM, axis=0, tiled=True
    )
    pieces = [feature] + [
        lax.ppermute(feature, "y", [(i, (i + k) % columns) for i in range(columns)]) for k in range(1, columns)
    ]
    feature_t = flip(pieces)
    block_grad = merge_tiles(
        tile_peer,
        tile_rel * block_count + tile_src,
        tile_count,
        tile_values,
        incoming,
        relations,
        block_count,
    )

    give = weight_terms(jnp.stack([1 - core, column]), feature_t, block_grad, relations)
    got = lax.ppermute(give, "core", [(0, 1), (1, 0)])
    keep = weight_terms(jnp.stack([core, column]), feature_t, block_grad, relations)
    j_count = keep.shape[1]
    mine = (keep + got).astype(BF).reshape(nx, half * j_count // nx, col_width)
    mine = fold(exchange(mine, "x"), None, 1)
    mine, late_grad, late_rows = lax.optimization_barrier((mine, block_grad, weight_rows))
    norm_scale = 1.0 / math.sqrt(row_count * partitions)
    mine = fold(exchange(mine.reshape(nz, -1, col_width), "z"), norm_scale, nz)
    mine = exchange(mine, "z").reshape(-1, col_width)
    mine = exchange(repeat(mine, nx), "x").reshape(-1, col_width)
    weight_grad = exchange(repeat(mine, 2), "core").reshape(relations, j_count, col_width)

    partial = feature_terms(late_grad, late_rows, columns)
    partial = lax.psum_scatter(partial, "y", scatter_dimension=0, tiled=True)[0]
    kind = node_type[:, None]
    gains = jnp.where(kind == 0, self_gain[0:1], jnp.where(kind == 1, self_gain[1:2], self_gain[2:3]))
    self_term = cotangent.astype(F32) * gains
    feature_grad = (partial + self_term).astype(BF)
    return (feature_grad, weight_grad)


def solution(mesh):
    fine = Mesh(mesh.devices.reshape(8, 4, 2, 8), ("z", "x", "core", "y"))
    return jax.shard_map(
        body,
        mesh=fine,
        in_specs=(
            P(DOM, "y"),
            P(DOM, "y"),
            P(DOM),
            P(None, "y"),
            P(None, DOM, "y"),
            P(DOM, None, None),
            P(DOM),
            P(DOM),
            P(DOM),
            P(DOM),
            P(DOM, None),
        ),
        out_specs=(P(DOM, "y"), P(None, None, "y")),
        check_vma=False,
    )
```

```python
import math

import jax
import jax.numpy as jnp
from jax import lax
from jax.experimental import pallas as pl
from jax.experimental.pallas import tpu as pltpu
from jax.sharding import Mesh, PartitionSpec as P

BF = jnp.bfloat16
F32 = jnp.float32
DOM = ("z", "x", "core")


def cost(flops, nbytes):
    return pl.CostEstimate(flops=flops, bytes_accessed=nbytes, transcendentals=0)


def whole():
    return pl.BlockSpec(memory_space=pltpu.VMEM)


def pick_blocks(wanted, blocks):
    count = wanted.shape[0]
    _, rows, cols = blocks.shape

    def kernel(want_ref, blk_ref, out_ref):
        for i in range(count):
            out_ref[i] = blk_ref[jnp.maximum(want_ref[i], 0)]

    return pl.pallas_call(
        kernel,
        out_shape=jax.ShapeDtypeStruct((count, rows, cols), blocks.dtype),
        in_specs=[pl.BlockSpec(memory_space=pltpu.SMEM), whole()],
        out_specs=whole(),
        cost_estimate=cost(0, count * rows * cols * 2),
        name="pick_blocks",
    )(wanted, blocks)


def merge_tiles(core, peer, slot, count, tiles, incoming, relations, block_count):
    slots, size, _ = tiles.shape
    cols = incoming.shape[2]
    half = relations // 2
    buckets = relations * block_count

    def kernel(core_ref, peer_ref, slot_ref, count_ref, tile_ref, inc_ref, keep_ref, give_ref, con, acc):
        acc[...] = jnp.zeros_like(acc)
        for t in range(slots):
            con[t] = lax.dot_general(
                tile_ref[t],
                inc_ref[peer_ref[t]],
                (((0,), (0,)), ((), ())),
                preferred_element_type=F32,
            )
        for t in range(slots):
            where = jnp.where(t < count_ref[0], slot_ref[t], buckets)
            acc[where] += con[t]
        first = core_ref[0] * (half * block_count)
        for ref, base in ((keep_ref, first), (give_ref, half * block_count - first)):
            for r in range(half):
                for b in range(block_count):
                    ref[b * size : (b + 1) * size, r * cols : (r + 1) * cols] = acc[base + r * block_count + b].astype(
                        BF
                    )

    smem = pl.BlockSpec(memory_space=pltpu.SMEM)
    return pl.pallas_call(
        kernel,
        out_shape=(jax.ShapeDtypeStruct((block_count * size, half * cols), BF),) * 2,
        in_specs=[smem, smem, smem, smem, whole(), whole()],
        out_specs=(whole(), whole()),
        scratch_shapes=[
            pltpu.VMEM((slots, size, cols), F32),
            pltpu.VMEM((buckets + 1, size, cols), F32),
        ],
        compiler_params=pltpu.CompilerParams(vmem_limit_bytes=24 << 20),
        cost_estimate=cost(2 * slots * size * size * cols, 4 << 20),
        name="merge_tiles",
    )(core, peer, slot, count, tiles, incoming)


def flip(column, pieces):
    n = len(pieces)
    rows, cols = pieces[0].shape

    def kernel(*refs):
        col_ref, out_ref = refs[0], refs[n + 1]
        for k in range(n):
            at = lax.rem(col_ref[0] - k + n, n)
            out_ref[pl.ds(pl.multiple_of(at * cols, cols), cols), :] = refs[k + 1][...].T

    return pl.pallas_call(
        kernel,
        out_shape=jax.ShapeDtypeStruct((n * cols, rows), pieces[0].dtype),
        in_specs=[pl.BlockSpec(memory_space=pltpu.SMEM)] + [whole()] * n,
        out_specs=whole(),
        cost_estimate=cost(0, 2 * n * rows * cols * 2),
        name="flip",
    )(column, *pieces)


def fold(parts, scale, copies):
    n, rows, cols = parts.shape

    def kernel(in_ref, out_ref):
        total = in_ref[0].astype(F32)
        for i in range(1, n):
            total = total + in_ref[i].astype(F32)
        if scale is not None:
            total = total * scale
        total = total.astype(BF)
        for i in range(copies):
            out_ref[i] = total

    return pl.pallas_call(
        kernel,
        out_shape=jax.ShapeDtypeStruct((copies, rows, cols), BF),
        in_specs=[whole()],
        out_specs=whole(),
        cost_estimate=cost(n * rows * cols, (n + copies) * rows * cols * 2),
        name="fold",
    )(parts)


def weight_terms(own_t, other_t, own_grad, other_grad, half):
    features, rows = own_t.shape
    wide = own_grad.shape[1]
    cols = wide // half
    group = 2

    def kernel(fa_ref, fb_ref, ga_ref, gb_ref, out_ref):
        d = jnp.dot(fa_ref[...], ga_ref[...], preferred_element_type=F32)
        d = d + jnp.dot(fb_ref[...], gb_ref[...], preferred_element_type=F32)
        for r in range(group):
            out_ref[r] = d[:, r * cols : (r + 1) * cols].astype(BF)

    grad_spec = pl.BlockSpec((rows, group * cols), lambda i: (0, i))
    return pl.pallas_call(
        kernel,
        out_shape=jax.ShapeDtypeStruct((half, features, cols), BF),
        grid=(half // group,),
        in_specs=[whole(), whole(), grad_spec, grad_spec],
        out_specs=pl.BlockSpec((group, features, cols), lambda i: (i, 0, 0)),
        compiler_params=pltpu.CompilerParams(vmem_limit_bytes=24 << 20),
        cost_estimate=cost(4 * features * rows * wide, 4 << 20),
        name="weight_terms",
    )(own_t, other_t, own_grad, other_grad)


def feature_terms(core, keep, give, weight_rows, n):
    rows, wide = keep.shape
    jw = weight_rows.shape[0] // n
    group = 2

    def kernel(core_ref, keep_ref, give_ref, w_ref, out_ref):
        first = pl.multiple_of(core_ref[0] * wide, wide)
        dims = (((1,), (1,)), ((), ()))
        d = lax.dot_general(keep_ref[...], w_ref[:, pl.ds(first, wide)], dims, preferred_element_type=F32)
        d = d + lax.dot_general(give_ref[...], w_ref[:, pl.ds(wide - first, wide)], dims, preferred_element_type=F32)
        for c in range(group):
            out_ref[c] = d[:, c * jw : (c + 1) * jw]

    return pl.pallas_call(
        kernel,
        out_shape=jax.ShapeDtypeStruct((n, rows, jw), F32),
        grid=(n // group,),
        in_specs=[
            pl.BlockSpec(memory_space=pltpu.SMEM),
            whole(),
            whole(),
            pl.BlockSpec((group * jw, 2 * wide), lambda c: (c, 0)),
        ],
        out_specs=pl.BlockSpec((group, rows, jw), lambda c: (c, 0, 0)),
        compiler_params=pltpu.CompilerParams(vmem_limit_bytes=24 << 20),
        cost_estimate=cost(4 * n * jw * rows * wide, 4 << 20),
        name="feature_terms",
    )(core, keep, give, weight_rows)


def exchange(parts, axis):
    return lax.all_to_all(parts, axis, split_axis=0, concat_axis=0, tiled=True)


def repeat(part, n):
    return jnp.broadcast_to(part[None], (n,) + part.shape)


def body(
    feature,
    cotangent,
    node_type,
    self_gain,
    weights,
    tile_values,
    tile_rel,
    tile_src,
    tile_peer,
    tile_count,
    send_block,
):
    partitions = lax.axis_size(DOM)
    row_count, col_width = cotangent.shape
    tile_size = tile_values.shape[1]
    block_count = row_count // tile_size
    relations, w_rows, _ = weights.shape
    half = relations // 2
    columns = lax.axis_size("y")
    nx = lax.axis_size("x")
    nz = lax.axis_size("z")
    core = lax.axis_index("core").astype(jnp.int32)[None]
    column = lax.axis_index("y").astype(jnp.int32)[None]
    swap = [(0, 1), (1, 0)]

    w_shard = weights.transpose(1, 0, 2).reshape(w_rows, relations * col_width)
    w_shard, wanted = lax.optimization_barrier((w_shard, send_block[0]))
    weight_rows = lax.all_gather(w_shard, DOM, axis=0, tiled=True)
    outgoing = pick_blocks(wanted, cotangent.reshape(block_count, tile_size, col_width))
    incoming = exchange(outgoing, DOM)
    pieces = [feature] + [
        lax.ppermute(feature, "y", [(i, (i + k) % columns) for i in range(columns)]) for k in range(1, columns)
    ]
    own_t = flip(column, pieces)
    other_t = lax.ppermute(own_t, "core", swap)
    keep, give = merge_tiles(
        core,
        tile_peer,
        tile_rel * block_count + tile_src,
        tile_count,
        tile_values,
        incoming,
        relations,
        block_count,
    )

    mine = weight_terms(own_t, other_t, keep, lax.ppermute(give, "core", swap), half)
    j_count = mine.shape[1]
    mine = mine.reshape(nx, half * j_count // nx, col_width)
    mine = fold(exchange(mine, "x"), None, 1)
    mine, late_keep, late_give, late_rows = lax.optimization_barrier((mine, keep, give, weight_rows))
    norm_scale = 1.0 / math.sqrt(row_count * partitions)
    mine = fold(exchange(mine.reshape(nz, -1, col_width), "z"), norm_scale, nz)
    mine = exchange(mine, "z").reshape(-1, col_width)
    mine = exchange(repeat(mine, nx), "x").reshape(-1, col_width)
    weight_grad = exchange(repeat(mine, 2), "core").reshape(relations, j_count, col_width)

    partial = feature_terms(core, late_keep, late_give, late_rows, columns)
    partial = lax.psum_scatter(partial, "y", scatter_dimension=0, tiled=True)[0]
    kind = node_type[:, None]
    gains = jnp.where(kind == 0, self_gain[0:1], jnp.where(kind == 1, self_gain[1:2], self_gain[2:3]))
    self_term = cotangent.astype(F32) * gains
    feature_grad = (partial + self_term).astype(BF)
    return (feature_grad, weight_grad)


def solution(mesh):
    fine = Mesh(mesh.devices.reshape(8, 4, 2, 8), ("z", "x", "core", "y"))
    return jax.shard_map(
        body,
        mesh=fine,
        in_specs=(
            P(DOM, "y"),
            P(DOM, "y"),
            P(DOM),
            P(None, "y"),
            P(None, DOM, "y"),
            P(DOM, None, None),
            P(DOM),
            P(DOM),
            P(DOM),
            P(DOM),
            P(DOM, None),
        ),
        out_specs=(P(DOM, "y"), P(None, None, "y")),
        check_vma=False,
    )
```

```python
import math

import jax
import jax.numpy as jnp
from jax import lax
from jax.experimental import pallas as pl
from jax.experimental.pallas import tpu as pltpu
from jax.sharding import Mesh, PartitionSpec as P

BF = jnp.bfloat16
F32 = jnp.float32
DOM = ("z", "x", "core")


def cost(flops, nbytes):
    return pl.CostEstimate(flops=flops, bytes_accessed=nbytes, transcendentals=0)


def whole():
    return pl.BlockSpec(memory_space=pltpu.VMEM)


def pick_blocks(wanted, blocks):
    count = wanted.shape[0]
    _, rows, cols = blocks.shape

    def kernel(want_ref, blk_ref, out_ref):
        for i in range(count):
            out_ref[i] = blk_ref[jnp.maximum(want_ref[i], 0)]

    return pl.pallas_call(
        kernel,
        out_shape=jax.ShapeDtypeStruct((count, rows, cols), blocks.dtype),
        in_specs=[pl.BlockSpec(memory_space=pltpu.SMEM), whole()],
        out_specs=whole(),
        cost_estimate=cost(0, count * rows * cols * 2),
        name="pick_blocks",
    )(wanted, blocks)


def merge_tiles(core, peer, slot, count, tiles, incoming, relations, block_count):
    slots, size, _ = tiles.shape
    cols = incoming.shape[2]
    half = relations // 2
    buckets = relations * block_count

    def kernel(core_ref, peer_ref, slot_ref, count_ref, tile_ref, inc_ref, keep_ref, give_ref, con, acc):
        acc[...] = jnp.zeros_like(acc)
        for t in range(slots):
            con[t] = lax.dot_general(
                tile_ref[t],
                inc_ref[peer_ref[t]],
                (((0,), (0,)), ((), ())),
                preferred_element_type=F32,
            )
        for t in range(slots):
            where = jnp.where(t < count_ref[0], slot_ref[t], buckets)
            acc[where] += con[t]
        first = core_ref[0] * (half * block_count)
        for ref, base in ((keep_ref, first), (give_ref, half * block_count - first)):
            for r in range(half):
                for b in range(block_count):
                    ref[b * size : (b + 1) * size, r * cols : (r + 1) * cols] = acc[base + r * block_count + b].astype(
                        BF
                    )

    smem = pl.BlockSpec(memory_space=pltpu.SMEM)
    return pl.pallas_call(
        kernel,
        out_shape=(jax.ShapeDtypeStruct((block_count * size, half * cols), BF),) * 2,
        in_specs=[smem, smem, smem, smem, whole(), whole()],
        out_specs=(whole(), whole()),
        scratch_shapes=[
            pltpu.VMEM((slots, size, cols), F32),
            pltpu.VMEM((buckets + 1, size, cols), F32),
        ],
        compiler_params=pltpu.CompilerParams(vmem_limit_bytes=12 << 20),
        cost_estimate=cost(2 * slots * size * size * cols, 4 << 20),
        name="merge_tiles",
    )(core, peer, slot, count, tiles, incoming)


def flip(column, pieces):
    n = sum(p.shape[0] for p in pieces)
    _, rows, cols = pieces[0].shape

    def kernel(*refs):
        col_ref, out_ref = refs[0], refs[-1]
        k = 0
        for ref in refs[1:-1]:
            for i in range(ref.shape[0]):
                at = jnp.bitwise_xor(col_ref[0], turned(k, n))
                out_ref[pl.ds(pl.multiple_of(at * cols, cols), cols), :] = ref[i].T
                k += 1

    return pl.pallas_call(
        kernel,
        out_shape=jax.ShapeDtypeStruct((n * cols, rows), pieces[0].dtype),
        in_specs=[pl.BlockSpec(memory_space=pltpu.SMEM)] + [whole()] * len(pieces),
        out_specs=whole(),
        compiler_params=pltpu.CompilerParams(vmem_limit_bytes=8 << 20),
        cost_estimate=cost(0, 2 * n * rows * cols * 2),
        name="flip",
    )(column, *pieces)


def turned(k, n):
    out, bit = 0, n // 2
    while bit:
        out += bit * (k % 2)
        k //= 2
        bit //= 2
    return out


def double(part, axis):
    n = lax.axis_size(axis)
    held, pieces, step = part[None], [part[None]], n // 2
    while step:
        got = lax.ppermute(held, axis, [(i, i ^ step) for i in range(n)])
        pieces.append(got)
        step //= 2
        if step:
            held = jnp.concatenate([held, got], axis=0)
    return pieces


def place(core, mine, other):
    rows, cols = mine.shape
    smem = pl.BlockSpec(memory_space=pltpu.SMEM)
    anywhere = pl.BlockSpec(memory_space=pl.ANY)

    def put(at_ref, part_ref, out_ref, sem):
        copy = pltpu.make_async_copy(part_ref, out_ref.at[at_ref[0]], sem)
        copy.start()
        copy.wait()

    def put_into(at_ref, part_ref, _, out_ref, sem):
        put(at_ref, part_ref, out_ref, sem)

    shape = jax.ShapeDtypeStruct((2, rows, cols), mine.dtype)
    half = pl.pallas_call(
        put,
        out_shape=shape,
        in_specs=[smem, whole()],
        out_specs=anywhere,
        scratch_shapes=[pltpu.SemaphoreType.DMA],
        compiler_params=pltpu.CompilerParams(vmem_limit_bytes=4 << 20),
        cost_estimate=cost(0, 2 * rows * cols * 2),
        name="place",
    )(core, mine)
    return pl.pallas_call(
        put_into,
        out_shape=shape,
        in_specs=[smem, whole(), anywhere],
        out_specs=anywhere,
        input_output_aliases={2: 0},
        scratch_shapes=[pltpu.SemaphoreType.DMA],
        compiler_params=pltpu.CompilerParams(vmem_limit_bytes=4 << 20),
        cost_estimate=cost(0, 2 * rows * cols * 2),
        name="place_into",
    )(1 - core, other, half)


def fold(parts, scale, copies):
    n, rows, cols = parts.shape

    def kernel(in_ref, out_ref):
        total = in_ref[0].astype(F32)
        for i in range(1, n):
            total = total + in_ref[i].astype(F32)
        if scale is not None:
            total = total * scale
        total = total.astype(BF)
        for i in range(copies):
            out_ref[i] = total

    return pl.pallas_call(
        kernel,
        out_shape=jax.ShapeDtypeStruct((copies, rows, cols), BF),
        in_specs=[whole()],
        out_specs=whole(),
        compiler_params=pltpu.CompilerParams(vmem_limit_bytes=8 << 20),
        cost_estimate=cost(n * rows * cols, (n + copies) * rows * cols * 2),
        name="fold",
    )(parts)


def weight_terms(own_t, other_t, own_grad, other_grad, half):
    features, rows = own_t.shape
    wide = own_grad.shape[1]
    cols = wide // half
    group = 2

    def kernel(fa_ref, fb_ref, ga_ref, gb_ref, out_ref):
        d = jnp.dot(fa_ref[...], ga_ref[...], preferred_element_type=F32)
        d = d + jnp.dot(fb_ref[...], gb_ref[...], preferred_element_type=F32)
        for r in range(group):
            out_ref[r] = d[:, r * cols : (r + 1) * cols].astype(BF)

    grad_spec = pl.BlockSpec((rows, group * cols), lambda i: (0, i))
    return pl.pallas_call(
        kernel,
        out_shape=jax.ShapeDtypeStruct((half, features, cols), BF),
        grid=(half // group,),
        in_specs=[whole(), whole(), grad_spec, grad_spec],
        out_specs=pl.BlockSpec((group, features, cols), lambda i: (i, 0, 0)),
        compiler_params=pltpu.CompilerParams(vmem_limit_bytes=12 << 20),
        cost_estimate=cost(4 * features * rows * wide, 4 << 20),
        name="weight_terms",
    )(own_t, other_t, own_grad, other_grad)


def feature_terms(core, keep, give, shards, n):
    rows, wide = keep.shape
    partitions, relations, w_rows, cols = shards.shape
    jw = partitions * w_rows // n
    group = 2
    each = partitions * group // n

    def kernel(core_ref, keep_ref, give_ref, w_ref, out_ref, w_all):
        for p in range(each):
            for r in range(relations):
                w_all[p * w_rows : (p + 1) * w_rows, r * cols : (r + 1) * cols] = w_ref[p, r]
        first = pl.multiple_of(core_ref[0] * wide, wide)
        dims = (((1,), (1,)), ((), ()))
        d = lax.dot_general(keep_ref[...], w_all[:, pl.ds(first, wide)], dims, preferred_element_type=F32)
        d = d + lax.dot_general(give_ref[...], w_all[:, pl.ds(wide - first, wide)], dims, preferred_element_type=F32)
        for g in range(group):
            out_ref[g] = d[:, g * jw : (g + 1) * jw]

    return pl.pallas_call(
        kernel,
        out_shape=jax.ShapeDtypeStruct((n, rows, jw), F32),
        grid=(n // group,),
        in_specs=[
            pl.BlockSpec(memory_space=pltpu.SMEM),
            whole(),
            whole(),
            pl.BlockSpec((each, relations, w_rows, cols), lambda c: (c, 0, 0, 0)),
        ],
        out_specs=pl.BlockSpec((group, rows, jw), lambda c: (c, 0, 0)),
        scratch_shapes=[pltpu.VMEM((group * jw, 2 * wide), BF)],
        compiler_params=pltpu.CompilerParams(vmem_limit_bytes=12 << 20),
        cost_estimate=cost(4 * n * jw * rows * wide, 4 << 20),
        name="feature_terms",
    )(core, keep, give, shards)


def exchange(parts, axis):
    return lax.all_to_all(parts, axis, split_axis=0, concat_axis=0, tiled=True)


def repeat(part, n):
    return jnp.broadcast_to(part[None], (n,) + part.shape)


def body(
    feature,
    cotangent,
    node_type,
    self_gain,
    weights,
    tile_values,
    tile_rel,
    tile_src,
    tile_peer,
    tile_count,
    send_block,
):
    partitions = lax.axis_size(DOM)
    row_count, col_width = cotangent.shape
    tile_size = tile_values.shape[1]
    block_count = row_count // tile_size
    relations = weights.shape[0]
    half = relations // 2
    columns = lax.axis_size("y")
    nx = lax.axis_size("x")
    nz = lax.axis_size("z")
    core = lax.axis_index("core").astype(jnp.int32)[None]
    column = lax.axis_index("y").astype(jnp.int32)[None]
    swap = [(0, 1), (1, 0)]

    shards = lax.all_gather(weights, DOM, axis=0)
    outgoing = pick_blocks(send_block[0], cotangent.reshape(block_count, tile_size, col_width))
    incoming = exchange(outgoing, DOM)
    pieces = double(feature, "y")
    own_t = flip(column, pieces)
    other_t = lax.ppermute(own_t, "core", swap)
    keep, give = merge_tiles(
        core,
        tile_peer,
        tile_rel * block_count + tile_src,
        tile_count,
        tile_values,
        incoming,
        relations,
        block_count,
    )

    mine = weight_terms(own_t, other_t, keep, lax.ppermute(give, "core", swap), half)
    j_count = mine.shape[1]
    mine = mine.reshape(nx, half * j_count // nx, col_width)
    mine = fold(exchange(mine, "x"), None, 1)
    mine, keep, give = lax.optimization_barrier((mine, keep, give))
    partial = feature_terms(core, keep, give, shards, columns)
    mine, partial = lax.optimization_barrier((exchange(mine.reshape(nz, -1, col_width), "z"), partial))
    partial = lax.psum_scatter(partial, "y", scatter_dimension=0, tiled=True)[0]
    norm_scale = 1.0 / math.sqrt(row_count * partitions)
    mine = fold(mine, norm_scale, nz)
    mine = exchange(mine, "z").reshape(-1, col_width)
    mine = exchange(repeat(mine, nx), "x").reshape(-1, col_width)

    weight_grad = place(core, mine, lax.ppermute(mine, "core", swap)).reshape(relations, j_count, col_width)

    kind = node_type[:, None]
    gains = jnp.where(kind == 0, self_gain[0:1], jnp.where(kind == 1, self_gain[1:2], self_gain[2:3]))
    self_term = cotangent.astype(F32) * gains
    feature_grad = (partial + self_term).astype(BF)
    return (feature_grad, weight_grad)


def solution(mesh):
    fine = Mesh(mesh.devices.reshape(8, 4, 2, 8), ("z", "x", "core", "y"))
    return jax.shard_map(
        body,
        mesh=fine,
        in_specs=(
            P(DOM, "y"),
            P(DOM, "y"),
            P(DOM),
            P(None, "y"),
            P(None, DOM, "y"),
            P(DOM, None, None),
            P(DOM),
            P(DOM),
            P(DOM),
            P(DOM),
            P(DOM, None),
        ),
        out_specs=(P(DOM, "y"), P(None, None, "y")),
        check_vma=False,
    )
```

```python
import math

import jax
import jax.numpy as jnp
from jax import lax
from jax.experimental import pallas as pl
from jax.experimental.pallas import tpu as pltpu
from jax.sharding import Mesh, PartitionSpec as P

BF = jnp.bfloat16
F32 = jnp.float32
DOM = ("z", "x", "core")
PLACE_HINT = 145 * 10**8


def cost(flops, nbytes):
    return pl.CostEstimate(flops=flops, bytes_accessed=nbytes, transcendentals=0)


def whole():
    return pl.BlockSpec(memory_space=pltpu.VMEM)


def pick_blocks(wanted, blocks):
    count = wanted.shape[0]
    _, rows, cols = blocks.shape

    def kernel(want_ref, blk_ref, out_ref):
        for i in range(count):
            out_ref[i] = blk_ref[jnp.maximum(want_ref[i], 0)]

    return pl.pallas_call(
        kernel,
        out_shape=jax.ShapeDtypeStruct((count, rows, cols), blocks.dtype),
        in_specs=[pl.BlockSpec(memory_space=pltpu.SMEM), whole()],
        out_specs=whole(),
        cost_estimate=cost(0, count * rows * cols * 2),
        name="pick_blocks",
    )(wanted, blocks)


def merge_tiles(core, peer, slot, count, tiles, incoming, relations, block_count):
    slots, size, _ = tiles.shape
    cols = incoming.shape[2]
    half = relations // 2
    buckets = relations * block_count

    def kernel(core_ref, peer_ref, slot_ref, count_ref, tile_ref, inc_ref, keep_ref, give_ref, con, acc):
        acc[...] = jnp.zeros_like(acc)
        for t in range(slots):
            con[t] = lax.dot_general(
                tile_ref[t],
                inc_ref[peer_ref[t]],
                (((0,), (0,)), ((), ())),
                preferred_element_type=F32,
            )
        for t in range(slots):
            where = jnp.where(t < count_ref[0], slot_ref[t], buckets)
            acc[where] += con[t]
        first = core_ref[0] * (half * block_count)
        for ref, base in ((keep_ref, first), (give_ref, half * block_count - first)):
            for r in range(half):
                for b in range(block_count):
                    ref[b * size : (b + 1) * size, r * cols : (r + 1) * cols] = acc[base + r * block_count + b].astype(
                        BF
                    )

    smem = pl.BlockSpec(memory_space=pltpu.SMEM)
    return pl.pallas_call(
        kernel,
        out_shape=(jax.ShapeDtypeStruct((block_count * size, half * cols), BF),) * 2,
        in_specs=[smem, smem, smem, smem, whole(), whole()],
        out_specs=(whole(), whole()),
        scratch_shapes=[
            pltpu.VMEM((slots, size, cols), F32),
            pltpu.VMEM((buckets + 1, size, cols), F32),
        ],
        compiler_params=pltpu.CompilerParams(vmem_limit_bytes=12 << 20),
        cost_estimate=cost(2 * slots * size * size * cols, 4 << 20),
        name="merge_tiles",
    )(core, peer, slot, count, tiles, incoming)


def flip(column, pieces):
    n = sum(p.shape[0] for p in pieces)
    _, rows, cols = pieces[0].shape

    def kernel(*refs):
        col_ref, out_ref = refs[0], refs[-1]
        k = 0
        for ref in refs[1:-1]:
            for i in range(ref.shape[0]):
                at = jnp.bitwise_xor(col_ref[0], turned(k, n))
                out_ref[pl.ds(pl.multiple_of(at * cols, cols), cols), :] = ref[i].T
                k += 1

    return pl.pallas_call(
        kernel,
        out_shape=jax.ShapeDtypeStruct((n * cols, rows), pieces[0].dtype),
        in_specs=[pl.BlockSpec(memory_space=pltpu.SMEM)] + [whole()] * len(pieces),
        out_specs=whole(),
        compiler_params=pltpu.CompilerParams(vmem_limit_bytes=8 << 20),
        cost_estimate=cost(0, 2 * n * rows * cols * 2),
        name="flip",
    )(column, *pieces)


def turned(k, n):
    out, bit = 0, n // 2
    while bit:
        out += bit * (k % 2)
        k //= 2
        bit //= 2
    return out


def double(part, axis):
    n = lax.axis_size(axis)
    held, pieces, step = part[None], [part[None]], n // 2
    while step:
        got = lax.ppermute(held, axis, [(i, i ^ step) for i in range(n)])
        pieces.append(got)
        step //= 2
        if step:
            held = jnp.concatenate([held, got], axis=0)
    return pieces


def place(core, mine, other):
    rows, cols = mine.shape
    smem = pl.BlockSpec(memory_space=pltpu.SMEM)
    anywhere = pl.BlockSpec(memory_space=pl.ANY)

    def put(at_ref, part_ref, out_ref, sem):
        copy = pltpu.make_async_copy(part_ref, out_ref.at[at_ref[0]], sem)
        copy.start()
        copy.wait()

    def put_into(at_ref, part_ref, _, out_ref, sem):
        put(at_ref, part_ref, out_ref, sem)

    shape = jax.ShapeDtypeStruct((2, rows, cols), mine.dtype)
    half = pl.pallas_call(
        put,
        out_shape=shape,
        in_specs=[smem, whole()],
        out_specs=anywhere,
        scratch_shapes=[pltpu.SemaphoreType.DMA],
        compiler_params=pltpu.CompilerParams(vmem_limit_bytes=4 << 20),
        cost_estimate=cost(PLACE_HINT, 2 * rows * cols * 2),
        name="place",
    )(core, mine)
    return pl.pallas_call(
        put_into,
        out_shape=shape,
        in_specs=[smem, whole(), anywhere],
        out_specs=anywhere,
        input_output_aliases={2: 0},
        scratch_shapes=[pltpu.SemaphoreType.DMA],
        compiler_params=pltpu.CompilerParams(vmem_limit_bytes=4 << 20),
        cost_estimate=cost(PLACE_HINT, 2 * rows * cols * 2),
        name="place_into",
    )(1 - core, other, half)


def fold(parts, scale, copies, after=None):
    n, rows, cols = parts.shape
    marks = [] if after is None else [after]

    def kernel(in_ref, *rest):
        out_ref = rest[-1]
        total = in_ref[0].astype(F32)
        for i in range(1, n):
            total = total + in_ref[i].astype(F32)
        if scale is not None:
            total = total * scale
        total = total.astype(BF)
        for i in range(copies):
            out_ref[i] = total

    return pl.pallas_call(
        kernel,
        out_shape=jax.ShapeDtypeStruct((copies, rows, cols), BF),
        in_specs=[whole()] + [pl.BlockSpec(memory_space=pl.ANY)] * len(marks),
        out_specs=whole(),
        compiler_params=pltpu.CompilerParams(vmem_limit_bytes=8 << 20),
        cost_estimate=cost(n * rows * cols, (n + copies) * rows * cols * 2),
        name="fold",
    )(parts, *marks)


def weight_terms(own_t, other_t, own_grad, other_grad, half):
    features, rows = own_t.shape
    wide = own_grad.shape[1]
    cols = wide // half
    group = 2

    def kernel(fa_ref, fb_ref, ga_ref, gb_ref, out_ref):
        d = jnp.dot(fa_ref[...], ga_ref[...], preferred_element_type=F32)
        d = d + jnp.dot(fb_ref[...], gb_ref[...], preferred_element_type=F32)
        for r in range(group):
            out_ref[r] = d[:, r * cols : (r + 1) * cols].astype(BF)

    grad_spec = pl.BlockSpec((rows, group * cols), lambda i: (0, i))
    return pl.pallas_call(
        kernel,
        out_shape=jax.ShapeDtypeStruct((half, features, cols), BF),
        grid=(half // group,),
        in_specs=[whole(), whole(), grad_spec, grad_spec],
        out_specs=pl.BlockSpec((group, features, cols), lambda i: (i, 0, 0)),
        compiler_params=pltpu.CompilerParams(vmem_limit_bytes=12 << 20),
        cost_estimate=cost(4 * features * rows * wide, 4 << 20),
        name="weight_terms",
    )(own_t, other_t, own_grad, other_grad)


def feature_terms(core, keep, give, shards, n):
    rows, wide = keep.shape
    partitions, relations, w_rows, cols = shards.shape
    jw = partitions * w_rows // n
    group = 2
    each = partitions * group // n

    def kernel(core_ref, keep_ref, give_ref, w_ref, out_ref, mark_ref, w_all):
        mark_ref[...] = jnp.zeros_like(mark_ref)
        for p in range(each):
            for r in range(relations):
                w_all[p * w_rows : (p + 1) * w_rows, r * cols : (r + 1) * cols] = w_ref[p, r]
        first = pl.multiple_of(core_ref[0] * wide, wide)
        dims = (((1,), (1,)), ((), ()))
        d = lax.dot_general(keep_ref[...], w_all[:, pl.ds(first, wide)], dims, preferred_element_type=F32)
        d = d + lax.dot_general(give_ref[...], w_all[:, pl.ds(wide - first, wide)], dims, preferred_element_type=F32)
        for g in range(group):
            out_ref[g] = d[:, g * jw : (g + 1) * jw]

    return pl.pallas_call(
        kernel,
        out_shape=(jax.ShapeDtypeStruct((n, rows, jw), F32), jax.ShapeDtypeStruct((8, 128), F32)),
        grid=(n // group,),
        in_specs=[
            pl.BlockSpec(memory_space=pltpu.SMEM),
            whole(),
            whole(),
            pl.BlockSpec((each, relations, w_rows, cols), lambda c: (c, 0, 0, 0)),
        ],
        out_specs=(
            pl.BlockSpec((group, rows, jw), lambda c: (c, 0, 0)),
            pl.BlockSpec((8, 128), lambda c: (0, 0)),
        ),
        scratch_shapes=[pltpu.VMEM((group * jw, 2 * wide), BF)],
        compiler_params=pltpu.CompilerParams(vmem_limit_bytes=12 << 20),
        cost_estimate=cost(4 * n * jw * rows * wide, 4 << 20),
        name="feature_terms",
    )(core, keep, give, shards)


def exchange(parts, axis):
    return lax.all_to_all(parts, axis, split_axis=0, concat_axis=0, tiled=True)


def repeat(part, n):
    return jnp.broadcast_to(part[None], (n,) + part.shape)


def body(
    feature,
    cotangent,
    node_type,
    self_gain,
    weights,
    tile_values,
    tile_rel,
    tile_src,
    tile_peer,
    tile_count,
    send_block,
):
    partitions = lax.axis_size(DOM)
    row_count, col_width = cotangent.shape
    tile_size = tile_values.shape[1]
    block_count = row_count // tile_size
    relations = weights.shape[0]
    half = relations // 2
    columns = lax.axis_size("y")
    nx = lax.axis_size("x")
    nz = lax.axis_size("z")
    core = lax.axis_index("core").astype(jnp.int32)[None]
    column = lax.axis_index("y").astype(jnp.int32)[None]
    swap = [(0, 1), (1, 0)]

    shards = lax.all_gather(weights, DOM, axis=0)
    outgoing = pick_blocks(send_block[0], cotangent.reshape(block_count, tile_size, col_width))
    incoming = exchange(outgoing, DOM)
    pieces = double(feature, "y")
    own_t = flip(column, pieces)
    kind = node_type[:, None]
    gains = jnp.where(kind == 0, self_gain[0:1], jnp.where(kind == 1, self_gain[1:2], self_gain[2:3]))
    self_term = cotangent.astype(F32) * gains
    own_t, self_term = lax.optimization_barrier((own_t, self_term))
    other_t = lax.ppermute(own_t, "core", swap)
    keep, give = merge_tiles(
        core,
        tile_peer,
        tile_rel * block_count + tile_src,
        tile_count,
        tile_values,
        incoming,
        relations,
        block_count,
    )

    mine = weight_terms(own_t, other_t, keep, lax.ppermute(give, "core", swap), half)
    j_count = mine.shape[1]
    mine = mine.reshape(nx, half * j_count // nx, col_width)
    mine = fold(exchange(mine, "x"), None, 1)
    mine, keep, give = lax.optimization_barrier((mine, keep, give))
    partial, mark = feature_terms(core, keep, give, shards, columns)
    mine = exchange(mine.reshape(nz, -1, col_width), "z")
    partial = lax.psum_scatter(partial, "y", scatter_dimension=0, tiled=True)[0]
    norm_scale = 1.0 / math.sqrt(row_count * partitions)
    mine = fold(mine, norm_scale, nz, mark)
    mine = exchange(mine, "z").reshape(-1, col_width)
    mine = exchange(repeat(mine, nx), "x").reshape(-1, col_width)
    weight_grad = place(core, mine, lax.ppermute(mine, "core", swap)).reshape(relations, j_count, col_width)

    feature_grad = (partial + self_term).astype(BF)
    return (feature_grad, weight_grad)


def solution(mesh):
    fine = Mesh(mesh.devices.reshape(8, 4, 2, 8), ("z", "x", "core", "y"))
    return jax.shard_map(
        body,
        mesh=fine,
        in_specs=(
            P(DOM, "y"),
            P(DOM, "y"),
            P(DOM),
            P(None, "y"),
            P(None, DOM, "y"),
            P(DOM, None, None),
            P(DOM),
            P(DOM),
            P(DOM),
            P(DOM),
            P(DOM, None),
        ),
        out_specs=(P(DOM, "y"), P(None, None, "y")),
        check_vma=False,
    )
```

```python
import math

import jax
import jax.numpy as jnp
from jax import lax
from jax.experimental import pallas as pl
from jax.experimental.pallas import tpu as pltpu
from jax.sharding import Mesh, PartitionSpec as P

BF = jnp.bfloat16
F32 = jnp.float32
DOM = ("z", "x", "core")
PLACE_HINT = 145 * 10**8


def cost(flops, nbytes):
    return pl.CostEstimate(flops=flops, bytes_accessed=nbytes, transcendentals=0)


def whole():
    return pl.BlockSpec(memory_space=pltpu.VMEM)


def pick_blocks(wanted, blocks):
    count = wanted.shape[0]
    _, rows, cols = blocks.shape

    def kernel(want_ref, blk_ref, out_ref):
        for i in range(count):
            out_ref[i] = blk_ref[jnp.maximum(want_ref[i], 0)]

    return pl.pallas_call(
        kernel,
        out_shape=jax.ShapeDtypeStruct((count, rows, cols), blocks.dtype),
        in_specs=[pl.BlockSpec(memory_space=pltpu.SMEM), whole()],
        out_specs=whole(),
        cost_estimate=cost(0, count * rows * cols * 2),
        name="pick_blocks",
    )(wanted, blocks)


def merge_tiles(core, peer, slot, count, tiles, incoming, relations, block_count):
    slots, size, _ = tiles.shape
    cols = incoming.shape[2]
    half = relations // 2
    buckets = relations * block_count

    def kernel(core_ref, peer_ref, slot_ref, count_ref, tile_ref, inc_ref, keep_ref, give_ref, con, acc):
        acc[...] = jnp.zeros_like(acc)
        for t in range(slots):
            con[t] = lax.dot_general(
                tile_ref[t],
                inc_ref[peer_ref[t]],
                (((0,), (0,)), ((), ())),
                preferred_element_type=F32,
            )
        for t in range(slots):
            where = jnp.where(t < count_ref[0], slot_ref[t], buckets)
            acc[where] += con[t]
        first = core_ref[0] * (half * block_count)
        for ref, base in ((keep_ref, first), (give_ref, half * block_count - first)):
            for r in range(half):
                for b in range(block_count):
                    ref[b * size : (b + 1) * size, r * cols : (r + 1) * cols] = acc[base + r * block_count + b].astype(
                        BF
                    )

    smem = pl.BlockSpec(memory_space=pltpu.SMEM)
    return pl.pallas_call(
        kernel,
        out_shape=(jax.ShapeDtypeStruct((block_count * size, half * cols), BF),) * 2,
        in_specs=[smem, smem, smem, smem, whole(), whole()],
        out_specs=(whole(), whole()),
        scratch_shapes=[
            pltpu.VMEM((slots, size, cols), F32),
            pltpu.VMEM((buckets + 1, size, cols), F32),
        ],
        compiler_params=pltpu.CompilerParams(vmem_limit_bytes=12 << 20),
        cost_estimate=cost(2 * slots * size * size * cols, 4 << 20),
        name="merge_tiles",
    )(core, peer, slot, count, tiles, incoming)


def flip(column, pieces):
    n = sum(p.shape[0] for p in pieces)
    _, rows, cols = pieces[0].shape

    def kernel(*refs):
        col_ref, out_ref = refs[0], refs[-1]
        k = 0
        for ref in refs[1:-1]:
            for i in range(ref.shape[0]):
                at = jnp.bitwise_xor(col_ref[0], turned(k, n))
                out_ref[pl.ds(pl.multiple_of(at * cols, cols), cols), :] = ref[i].T
                k += 1

    return pl.pallas_call(
        kernel,
        out_shape=jax.ShapeDtypeStruct((n * cols, rows), pieces[0].dtype),
        in_specs=[pl.BlockSpec(memory_space=pltpu.SMEM)] + [whole()] * len(pieces),
        out_specs=whole(),
        compiler_params=pltpu.CompilerParams(vmem_limit_bytes=8 << 20),
        cost_estimate=cost(0, 2 * n * rows * cols * 2),
        name="flip",
    )(column, *pieces)


def turned(k, n):
    out, bit = 0, n // 2
    while bit:
        out += bit * (k % 2)
        k //= 2
        bit //= 2
    return out


def double(part, axis):
    n = lax.axis_size(axis)
    held, pieces, step = part[None], [part[None]], n // 2
    while step:
        got = lax.ppermute(held, axis, [(i, i ^ step) for i in range(n)])
        pieces.append(got)
        step //= 2
        if step:
            held = jnp.concatenate([held, got], axis=0)
    return pieces


def place(core, mine, other):
    rows, cols = mine.shape
    smem = pl.BlockSpec(memory_space=pltpu.SMEM)
    anywhere = pl.BlockSpec(memory_space=pl.ANY)

    def put(at_ref, part_ref, out_ref, sem):
        copy = pltpu.make_async_copy(part_ref, out_ref.at[at_ref[0]], sem)
        copy.start()
        copy.wait()

    def put_into(at_ref, part_ref, _, out_ref, sem):
        put(at_ref, part_ref, out_ref, sem)

    shape = jax.ShapeDtypeStruct((2, rows, cols), mine.dtype)
    half = pl.pallas_call(
        put,
        out_shape=shape,
        in_specs=[smem, whole()],
        out_specs=anywhere,
        scratch_shapes=[pltpu.SemaphoreType.DMA],
        compiler_params=pltpu.CompilerParams(vmem_limit_bytes=4 << 20),
        cost_estimate=cost(PLACE_HINT, 2 * rows * cols * 2),
        name="place",
    )(core, mine)
    return pl.pallas_call(
        put_into,
        out_shape=shape,
        in_specs=[smem, whole(), anywhere],
        out_specs=anywhere,
        input_output_aliases={2: 0},
        scratch_shapes=[pltpu.SemaphoreType.DMA],
        compiler_params=pltpu.CompilerParams(vmem_limit_bytes=4 << 20),
        cost_estimate=cost(PLACE_HINT, 2 * rows * cols * 2),
        name="place_into",
    )(1 - core, other, half)


def fold(parts, scale, copies, after=None):
    n, rows, cols = parts.shape
    marks = [] if after is None else [after]

    def kernel(in_ref, *rest):
        out_ref = rest[-1]
        total = in_ref[0].astype(F32)
        for i in range(1, n):
            total = total + in_ref[i].astype(F32)
        if scale is not None:
            total = total * scale
        total = total.astype(BF)
        for i in range(copies):
            out_ref[i] = total

    return pl.pallas_call(
        kernel,
        out_shape=jax.ShapeDtypeStruct((copies, rows, cols), BF),
        in_specs=[whole()] + [pl.BlockSpec(memory_space=pl.ANY)] * len(marks),
        out_specs=whole(),
        compiler_params=pltpu.CompilerParams(vmem_limit_bytes=8 << 20),
        cost_estimate=cost(n * rows * cols, (n + copies) * rows * cols * 2),
        name="fold",
    )(parts, *marks)


def weight_terms(own_t, other_t, own_grad, other_grad, half):
    features, rows = own_t.shape
    wide = own_grad.shape[1]
    cols = wide // half
    group = 2

    def kernel(fa_ref, fb_ref, ga_ref, gb_ref, out_ref):
        d = jnp.dot(fa_ref[...], ga_ref[...], preferred_element_type=F32)
        d = d + jnp.dot(fb_ref[...], gb_ref[...], preferred_element_type=F32)
        for r in range(group):
            out_ref[r] = d[:, r * cols : (r + 1) * cols].astype(BF)

    grad_spec = pl.BlockSpec((rows, group * cols), lambda i: (0, i))
    return pl.pallas_call(
        kernel,
        out_shape=jax.ShapeDtypeStruct((half, features, cols), BF),
        grid=(half // group,),
        in_specs=[whole(), whole(), grad_spec, grad_spec],
        out_specs=pl.BlockSpec((group, features, cols), lambda i: (i, 0, 0)),
        compiler_params=pltpu.CompilerParams(vmem_limit_bytes=12 << 20),
        cost_estimate=cost(4 * features * rows * wide, 4 << 20),
        name="weight_terms",
    )(own_t, other_t, own_grad, other_grad)


def feature_terms(core, keep, give, shards, n):
    rows, wide = keep.shape
    partitions, relations, w_rows, cols = shards.shape
    jw = partitions * w_rows // n
    group = 2
    each = partitions * group // n

    def kernel(core_ref, keep_ref, give_ref, w_ref, out_ref, mark_ref, w_all):
        mark_ref[...] = jnp.zeros_like(mark_ref)
        for p in range(each):
            for r in range(relations):
                w_all[p * w_rows : (p + 1) * w_rows, r * cols : (r + 1) * cols] = w_ref[p, r]
        first = pl.multiple_of(core_ref[0] * wide, wide)
        dims = (((1,), (1,)), ((), ()))
        d = lax.dot_general(keep_ref[...], w_all[:, pl.ds(first, wide)], dims, preferred_element_type=F32)
        d = d + lax.dot_general(give_ref[...], w_all[:, pl.ds(wide - first, wide)], dims, preferred_element_type=F32)
        for g in range(group):
            out_ref[g] = d[:, g * jw : (g + 1) * jw]

    return pl.pallas_call(
        kernel,
        out_shape=(jax.ShapeDtypeStruct((n, rows, jw), F32), jax.ShapeDtypeStruct((8, 128), F32)),
        grid=(n // group,),
        in_specs=[
            pl.BlockSpec(memory_space=pltpu.SMEM),
            whole(),
            whole(),
            pl.BlockSpec((each, relations, w_rows, cols), lambda c: (c, 0, 0, 0)),
        ],
        out_specs=(
            pl.BlockSpec((group, rows, jw), lambda c: (c, 0, 0)),
            pl.BlockSpec((8, 128), lambda c: (0, 0)),
        ),
        scratch_shapes=[pltpu.VMEM((group * jw, 2 * wide), BF)],
        cost_estimate=cost(4 * n * jw * rows * wide, 4 << 20),
        name="feature_terms",
    )(core, keep, give, shards)


def exchange(parts, axis):
    return lax.all_to_all(parts, axis, split_axis=0, concat_axis=0, tiled=True)


def repeat(part, n):
    return jnp.broadcast_to(part[None], (n,) + part.shape)


def body(
    feature,
    cotangent,
    node_type,
    self_gain,
    weights,
    tile_values,
    tile_rel,
    tile_src,
    tile_peer,
    tile_count,
    send_block,
):
    partitions = lax.axis_size(DOM)
    row_count, col_width = cotangent.shape
    tile_size = tile_values.shape[1]
    block_count = row_count // tile_size
    relations = weights.shape[0]
    half = relations // 2
    columns = lax.axis_size("y")
    nx = lax.axis_size("x")
    nz = lax.axis_size("z")
    core = lax.axis_index("core").astype(jnp.int32)[None]
    column = lax.axis_index("y").astype(jnp.int32)[None]
    swap = [(0, 1), (1, 0)]

    shards = lax.all_gather(weights, DOM, axis=0)
    outgoing = pick_blocks(send_block[0], cotangent.reshape(block_count, tile_size, col_width))
    incoming = exchange(outgoing, DOM)
    pieces = double(feature, "y")
    own_t = flip(column, pieces)
    kind = node_type[:, None]
    gains = jnp.where(kind == 0, self_gain[0:1], jnp.where(kind == 1, self_gain[1:2], self_gain[2:3]))
    self_term = cotangent.astype(F32) * gains
    own_t, self_term = lax.optimization_barrier((own_t, self_term))
    other_t = lax.ppermute(own_t, "core", swap)
    keep, give = merge_tiles(
        core,
        tile_peer,
        tile_rel * block_count + tile_src,
        tile_count,
        tile_values,
        incoming,
        relations,
        block_count,
    )

    mine = weight_terms(own_t, other_t, keep, lax.ppermute(give, "core", swap), half)
    j_count = mine.shape[1]
    mine = mine.reshape(nx, half * j_count // nx, col_width)
    mine = fold(exchange(mine, "x"), None, 1)
    mine, keep, give = lax.optimization_barrier((mine, keep, give))
    partial, mark = feature_terms(core, keep, give, shards, columns)
    mine = exchange(mine.reshape(nz, -1, col_width), "z")
    partial = lax.psum_scatter(partial, "y", scatter_dimension=0, tiled=True)[0]
    norm_scale = 1.0 / math.sqrt(row_count * partitions)
    mine = fold(mine, norm_scale, nz, mark)
    mine = exchange(mine, "z").reshape(-1, col_width)
    mine = exchange(repeat(mine, nx), "x").reshape(-1, col_width)
    weight_grad = place(core, mine, lax.ppermute(mine, "core", swap)).reshape(relations, j_count, col_width)

    feature_grad = (partial + self_term).astype(BF)
    return (feature_grad, weight_grad)


def solution(mesh):
    fine = Mesh(mesh.devices.reshape(8, 4, 2, 8), ("z", "x", "core", "y"))
    return jax.shard_map(
        body,
        mesh=fine,
        in_specs=(
            P(DOM, "y"),
            P(DOM, "y"),
            P(DOM),
            P(None, "y"),
            P(None, DOM, "y"),
            P(DOM, None, None),
            P(DOM),
            P(DOM),
            P(DOM),
            P(DOM),
            P(DOM, None),
        ),
        out_specs=(P(DOM, "y"), P(None, None, "y")),
        check_vma=False,
    )
```
